32 devices in a mesh: groups: 2 (over y), rec: 4 (over z), lig: 2 (over x), fft: 2 (over core).
Axes of the slice: x: 2, y: 2, z: 4, core: 2. Of those that a mesh axis runs over, the one named last changes fastest.
Arguments:
- receptor_occupancy: int32 [16, 4, 64, 4096], P(('groups', 'rec', 'lig'), None, 'fft'), parts along dimension 0, may hold values from 0 to 3
- ligand_occupancy: int32 [16, 4, 64, 4096], P(('groups', 'rec', 'lig'), None, 'fft'), parts along dimension 0, may hold values from 0 to 3
- rot_index: int32 [16], P(('groups', 'rec', 'lig')), parts along dimension 0, may hold values from 0 to 3
- receptor_extent: int32 [16], P(('groups', 'rec', 'lig')), parts along dimension 0, may hold values from 16 to 64, as said below
- channel_weight: float32 [4], replicated, may hold values from -1 to 2
Outputs:
- plane_top: float32 [16, 3, 2, 64], P(('groups', 'rec', 'lig'), None, None, 'fft'), parts along dimension 0
The draws below stay inside these ranges and needn't reach their ends.
There are 2 independent parts, one for each index of `groups`. The reference program is written for one: setup_inputs(seed, part) draws one part's arguments, and reference() takes and returns one part's arrays. A program takes and returns all parts, laid end to end along the dimension named above; an argument that names none is the same for every part. Nothing has to cross between parts.
Inputs may be any that keep to these rules, and one draw needn't show every extreme that they name: `rot_index`: quarter turns. `receptor_extent`: some receptor has extent 64.
All inputs are finite; a program needn't handle non-finite values.
Results may differ from the reference program's by a relative error of at most 0.0062.
Values may be sent and summed in bfloat16 or wider, within the bound.
A program may use at most 128 MiB of HBM per device.

```python
import math
from functools import partial
import jax
import jax.numpy as jnp
from jax import lax

G = 64
C = 4
REC_STEPS = 3
LIG_STEPS = 2
RECS = 8
POSES = 8
N_REC = 4
N_LIG = 2


def draw_receptor_extent(key, part):
    extents = jax.random.randint(key, (RECS,), G // 4, G + 1)
    chosen = jax.random.randint(jax.random.fold_in(key, 7), (), 0, RECS)
    return jnp.where(jnp.arange(RECS) == chosen, G, extents).astype(jnp.int32)


def set_ends(entries, rng, smallest, largest):
    longest = entries.shape.index(max(entries.shape))
    spots = []
    for shift in (0, 1):
        where = [jax.random.randint(jax.random.fold_in(rng, axis), (), 0, length) for axis, length in enumerate(entries.shape)]
        where[longest] = (where[longest] + shift) % entries.shape[longest]
        spots.append(tuple(where))
    return entries.at[spots[0]].set(smallest).at[spots[1]].set(largest)


def setup_inputs(seed: int = 0, part: int = 0) -> dict:
    arg_keys = jax.random.split(jax.random.key(seed), 6)
    own_keys = jax.random.split(jax.random.fold_in(arg_keys[5], part), 6)
    return {
        "receptor_occupancy": set_ends(jax.random.randint(own_keys[0], (RECS, C, G, G * G), 0, 4), jax.random.fold_in(own_keys[0], 1), 0, 3).astype(jnp.int32),
        "ligand_occupancy": set_ends(jax.random.randint(own_keys[1], (POSES, C, G, G * G), 0, 4), jax.random.fold_in(own_keys[1], 1), 0, 3).astype(jnp.int32),
        "rot_index": set_ends(jax.random.randint(own_keys[2], (POSES,), 0, 4), jax.random.fold_in(own_keys[2], 1), 0, 3).astype(jnp.int32),
        "receptor_extent": draw_receptor_extent(jax.random.fold_in(jax.random.fold_in(arg_keys[5], part), 71), part),
        "channel_weight": jnp.clip(jax.random.uniform(arg_keys[4], (C,), jnp.float32, -1.0, 2.0), -1.0, 2.0),
    }


def trig_tables(cells):
    indices = jnp.arange(cells, dtype=jnp.int32)
    phases = indices[:, None] * indices[None, :] % cells
    angles = phases.astype(jnp.float32) * (2.0 * math.pi / cells)
    return (jnp.cos(angles), jnp.sin(angles))

def mixing(cosine_table, sine_table, direction):
    row_real = jnp.stack([cosine_table, -direction * sine_table], axis=-1)
    row_imag = jnp.stack([direction * sine_table, cosine_table], axis=-1)
    return jnp.stack([row_real, row_imag], axis=-2)

def rounded(values):
    return lax.optimization_barrier(values.astype(jnp.bfloat16)).astype(jnp.float32)

def rotate_quarter(occupancy, turns):
    branches = [partial(jnp.rot90, k=quarter, axes=(2, 3)) for quarter in range(4)]
    return lax.switch(turns, branches, occupancy)

def unfold_grid(occupancy):
    cells = occupancy.shape[1]
    return occupancy.reshape(occupancy.shape[0], cells, cells, cells)

def forward_grid(occupancy, z_forward, forward_mix):
    channels = occupancy.shape[0]
    cells = occupancy.shape[-1]
    values = occupancy.astype(jnp.float32)
    section_one = rounded(jnp.einsum('cxyz,zw->cxyw', values, z_forward))
    section_one = section_one.reshape(channels, cells, cells, 2, cells)
    section_two = rounded(jnp.einsum('cxypz,kyqp->cxkqz', section_one, forward_mix))
    section_three = jnp.einsum('cxbpz,kxqp->ckbqz', section_two, forward_mix)
    return section_three.astype(jnp.bfloat16).reshape(channels, cells, cells, 2 * cells)

def cross_spectrum(receptor, ligand, weights, nonzero, volume):
    cells = receptor.shape[1]
    receptor = receptor.astype(jnp.float32)
    ligand = ligand.astype(jnp.float32)
    rec_real = receptor[..., :cells]
    rec_imag = receptor[..., cells:]
    lig_real = ligand[..., :cells]
    lig_imag = ligand[..., cells:]
    scaled = weights[:, None, None, None]
    real_part = lax.optimization_barrier(jnp.sum(scaled * (rec_real * lig_real + rec_imag * lig_imag), axis=0))
    imag_part = lax.optimization_barrier(jnp.sum(scaled * (rec_imag * lig_real - rec_real * lig_imag), axis=0))
    joined = jnp.concatenate([real_part, imag_part], axis=-1) * volume
    return rounded(jnp.where(nonzero, joined, 0.0))

def inverse_pair(cross, extent_now, inverse_mix, z_inverse, real_rows, score_scale):
    cells = cross.shape[0]
    spread = cross.reshape(cells, cells, 2, cells)
    back_one = rounded(jnp.einsum('xbpz,nxqp->nbqz', spread, inverse_mix)).reshape(cells, cells, 2 * cells)
    back_two = rounded(jnp.einsum('xbw,wv->xbv', back_one, z_inverse)).reshape(cells, cells, 2, cells)
    scores = jnp.einsum('xkpz,ykp->xyz', back_two, real_rows) * score_scale
    plane_max = lax.optimization_barrier(jnp.max(scores, axis=(1, 2)))
    planes = jnp.arange(cells, dtype=jnp.int32)
    return jnp.where(planes < extent_now, plane_max, 0.0)

def reference(receptor_occupancy, ligand_occupancy, rot_index, receptor_extent, channel_weight):
    cells = G
    cosine_table, sine_table = trig_tables(cells)
    forward_mix = rounded(mixing(cosine_table, sine_table, -1.0))
    inverse_mix = rounded(mixing(cosine_table, sine_table, 1.0))
    z_forward = rounded(jnp.concatenate([cosine_table, -sine_table], axis=1))
    z_inverse = jnp.transpose(inverse_mix, (3, 1, 2, 0)).reshape(2 * cells, 2 * cells)
    real_rows = inverse_mix[:, :, 0, :]
    volume = 1.0 / float(cells) ** 3
    score_scale = 1.0 / (cells * math.sqrt(cells))
    kx_index = lax.broadcasted_iota(jnp.int32, (cells, cells, 2 * cells), 0)
    ky_index = lax.broadcasted_iota(jnp.int32, (cells, cells, 2 * cells), 1)
    kz_index = lax.broadcasted_iota(jnp.int32, (cells, cells, 2 * cells), 2) % cells
    nonzero = kx_index + ky_index + kz_index > 0

    def receptor_spectrum(occupancy):
        return forward_grid(unfold_grid(occupancy), z_forward, forward_mix)

    def pose_spectrum(pose_pair):
        occupancy, turns = pose_pair
        return forward_grid(rotate_quarter(unfold_grid(occupancy), turns), z_forward, forward_mix)
    receptor_spectra = lax.map(receptor_spectrum, receptor_occupancy)
    pose_spectra = lax.map(pose_spectrum, (ligand_occupancy, rot_index))

    def device_row(position):
        cycle_row = position // N_LIG
        cycle_col = position % N_LIG
        outputs = []
        for rec_step in range(REC_STEPS):
            receptor_index = ((cycle_row - rec_step) % N_REC * N_LIG + cycle_col).astype(jnp.int32)
            receptor = receptor_spectra[receptor_index]
            extent_now = receptor_extent[receptor_index]
            row_scores = []
            for lig_step in range(LIG_STEPS):
                pose_index = (cycle_row * N_LIG + (cycle_col - lig_step) % N_LIG).astype(jnp.int32)
                cross = cross_spectrum(receptor, pose_spectra[pose_index], channel_weight, nonzero, volume)
                row_scores.append(inverse_pair(cross, extent_now, inverse_mix, z_inverse, real_rows, score_scale))
            outputs.append(jnp.stack(row_scores))
        return jnp.stack(outputs)
    return lax.map(device_row, jnp.arange(N_REC * N_LIG, dtype=jnp.int32))
```

```python
import math

import jax
import jax.numpy as jnp
import numpy as np
from jax import lax
from jax.experimental import pallas as pl
from jax.experimental.pallas import tpu as pltpu
from jax.sharding import PartitionSpec as P

REC_STEPS = 3
LIG_STEPS = 2
F32 = jnp.float32
BF16 = jnp.bfloat16


def passed_along(value, axis, steps):
    count = lax.axis_size(axis)
    pairs = [(source, (source + steps) % count) for source in range(count)]
    return lax.ppermute(value, axis, pairs)


def trig_tables(cells):
    indices = np.arange(cells)
    phases = indices[:, None] * indices[None, :] % cells
    angles = phases.astype(np.float32) * np.float32(2.0 * math.pi / cells)
    return np.cos(angles), np.sin(angles)


def lane_mixes(real, imag):
    first = np.block([[real, imag], [-imag, real]])
    second = np.block([[-imag, real], [-real, -imag]])
    return np.stack([first, second])


def make_tables(cells, half, padded):
    cosine, sine = trig_tables(cells)
    split = cells // 2
    x_rows = np.zeros((2 * padded, cells), np.float32)
    x_rows[:half] = cosine[:half]
    x_rows[padded : padded + half] = -sine[:half]
    x_swapped = np.concatenate([x_rows[:, split:], x_rows[:, :split]], axis=1)
    y_rows = np.concatenate([cosine, -sine], axis=0)
    forward = (
        np.stack([x_rows, x_swapped]),
        np.stack([y_rows, y_rows[:, ::-1]]),
        np.stack([lane_mixes(cosine, -sine), lane_mixes(cosine[::-1], -sine[::-1])]),
    )
    twice = np.full((half,), 2.0, np.float32)
    twice[0] = 1.0
    twice[-1] = 1.0
    x_back = np.zeros((cells, 2 * padded), np.float32)
    x_back[:, :half] = cosine[:, :half] * twice
    x_back[:, padded : padded + half] = -sine[:, :half] * twice
    backward = (
        x_back,
        np.concatenate([cosine, sine], axis=0),
        lane_mixes(cosine, sine),
    )
    return (
        tuple(jnp.asarray(table, BF16) for table in forward),
        tuple(jnp.asarray(table, BF16) for table in backward),
    )


def group_of(half):
    return max(size for size in range(1, 12) if half % size == 0)


def plane_transform(tiles, y_rows, mixes):
    cells, lanes = tiles[0].shape
    mixed = jnp.dot(y_rows, jnp.concatenate(tiles, axis=1), preferred_element_type=F32)
    mixed = mixed.astype(BF16)
    parts = [mixed[:, n * lanes : (n + 1) * lanes] for n in range(len(tiles))]
    real = jnp.concatenate([part[:cells] for part in parts], axis=0)
    imag = jnp.concatenate([part[cells:] for part in parts], axis=0)
    return jnp.dot(real, mixes[0], preferred_element_type=F32) + jnp.dot(
        imag, mixes[1], preferred_element_type=F32
    )


def forward_kernel(half, padded, sel, own, received, x_rows, y_rows, mixes, out, tiles):
    cells = y_rows.shape[2]
    lanes = 2 * cells
    group = group_of(half)
    grid = jnp.concatenate([own[0, 0].astype(F32).astype(BF16), received[0]], axis=0)
    low = lax.broadcasted_iota(jnp.int32, (padded, lanes), 1) < cells
    wide = 8 * lanes
    for block in range(cells * cells // wide):
        rows = jnp.dot(
            x_rows[0], grid[:, block * wide : (block + 1) * wide], preferred_element_type=F32
        )
        for piece in range(wide // lanes):
            real = rows[:padded, piece * lanes : (piece + 1) * lanes]
            imag = rows[padded:, piece * lanes : (piece + 1) * lanes]
            y = 2 * (block * (wide // lanes) + piece)
            tiles[pl.ds(y, padded, stride=cells), :] = jnp.where(
                low, real, pltpu.roll(imag, cells, 1)
            )
            tiles[pl.ds(y + 1, padded, stride=cells), :] = jnp.where(
                low, pltpu.roll(real, cells, 1), imag
            )

    def tile_at(k):
        return pl.ds(pl.multiple_of(k * cells, cells), cells)

    @pl.when(sel[3] == 1)
    def _():
        def turn(step, carry):
            for n in range(group):
                where = tile_at(step * group + n)
                turned = jnp.transpose(tiles[where, :])
                tiles[where, :] = jnp.concatenate([turned[:cells], turned[cells:]], axis=1)
            return carry

        lax.fori_loop(0, half // group, turn, 0)

    def body(step, carry):
        loaded = [tiles[tile_at(step * group + n), :].astype(BF16) for n in range(group)]
        done = plane_transform(loaded, y_rows[0], mixes[0])
        out[0, pl.ds(step * group, group)] = done.astype(BF16).reshape(group, cells, lanes)
        return carry

    lax.fori_loop(0, half // group, body, 0)


def forward(occupancy, received, sel, tables, half, padded):
    mine, thickness, plane = received.shape
    cells = tables[1].shape[2]
    lanes = 2 * cells
    grid_spec = pltpu.PrefetchScalarGridSpec(
        num_scalar_prefetch=1,
        grid=(mine,),
        in_specs=[
            pl.BlockSpec((1, 1, thickness, plane), lambda c, s: (0, s[0] * mine + c, 0, 0)),
            pl.BlockSpec((1, thickness, plane), lambda c, s: (c, 0, 0)),
            pl.BlockSpec((1, 2 * padded, cells), lambda c, s: (s[0], 0, 0)),
            pl.BlockSpec((1, lanes, cells), lambda c, s: (s[1], 0, 0)),
            pl.BlockSpec((1, 2, lanes, lanes), lambda c, s: (s[2], 0, 0, 0)),
        ],
        out_specs=pl.BlockSpec((1, half, cells, lanes), lambda c, s: (c, 0, 0, 0)),
        scratch_shapes=[pltpu.VMEM((padded * cells, lanes), F32)],
    )
    return pl.pallas_call(
        lambda *refs: forward_kernel(half, padded, *refs),
        out_shape=jax.ShapeDtypeStruct((mine, half, cells, lanes), BF16),
        grid_spec=grid_spec,
        name="forward_grid",
        cost_estimate=pl.CostEstimate(
            flops=mine * half * 6 * lanes * lanes * cells,
            bytes_accessed=mine * plane * thickness * 20,
            transcendentals=0,
        ),
    )(sel, occupancy, received, *tables)


def partial_cross(base, weights, receptor, ligand, where, cells):
    same = None
    swapped = None
    for channel in range(receptor.shape[0]):
        weight = weights[base + channel]
        left = receptor[channel, where].astype(F32) * weight
        right = ligand(channel, where).astype(F32)
        turned = pltpu.roll(right, cells, right.ndim - 1)
        same = left * right if same is None else same + left * right
        swapped = left * turned if swapped is None else swapped + left * turned
    axis = same.ndim - 1
    low = lax.broadcasted_iota(jnp.int32, same.shape, axis) < cells
    real = same + pltpu.roll(same, cells, axis)
    imag = swapped - pltpu.roll(swapped, cells, axis)
    return jnp.where(low, real, imag)


def chosen(pick_second, first, second):
    def read(channel, where):
        return jnp.where(pick_second, second[channel, where], first[channel, where])

    return read


def send_kernel(core, weights, receptor, first, second, out):
    cells = receptor.shape[2]
    half = receptor.shape[1]
    base = core[0] * receptor.shape[0]
    other = chosen(core[0] == 0, first, second)

    def body(k, carry):
        out[k] = partial_cross(base, weights, receptor, other, k, cells).astype(BF16)
        return carry

    lax.fori_loop(0, half, body, 0)


def vmem():
    return pl.BlockSpec(memory_space=pltpu.VMEM)


def smem():
    return pl.BlockSpec(memory_space=pltpu.SMEM)


def send_part(core, weights, receptor, first, second):
    mine, half, cells, lanes = receptor.shape
    return pl.pallas_call(
        send_kernel,
        out_shape=jax.ShapeDtypeStruct((half, cells, lanes), BF16),
        in_specs=[smem(), smem(), vmem(), vmem(), vmem()],
        out_specs=vmem(),
        name="cross_send",
        cost_estimate=pl.CostEstimate(
            flops=mine * half * cells * lanes * 10,
            bytes_accessed=half * cells * lanes * 14,
            transcendentals=0,
        ),
    )(core, weights, receptor, first, second)


def inverse_kernel(
    padded, core, weights, receptor, first, second, arrived, x_back, y_rows, mixes, out, tiles, lined
):
    mine, half, cells, lanes = receptor.shape
    group = group_of(half)
    base = core[0] * mine
    ours = chosen(core[0] == 1, first, second)
    tiles[half * cells :, :] = jnp.zeros(((padded - half) * cells, lanes), F32)
    row = lax.broadcasted_iota(jnp.int32, (cells, lanes), 0)
    lane = lax.broadcasted_iota(jnp.int32, (cells, lanes), 1) % cells
    origin = row + lane

    def body(step, carry):
        loaded = []
        for n in range(group):
            k = step * group + n
            cross = partial_cross(base, weights, receptor, ours, k, cells)
            cross = cross + arrived[k].astype(F32)
            loaded.append(jnp.where(origin + k > 0, cross, 0.0).astype(BF16))
        done = plane_transform(loaded, y_rows[...], mixes[...])
        size = group * cells
        tiles[pl.ds(pl.multiple_of(step * size, size), size), :] = done
        return carry

    lax.fori_loop(0, half // group, body, 0)
    low = lax.broadcasted_iota(jnp.int32, (padded, lanes), 1) < cells
    for y in range(0, cells, 2):
        even = tiles[pl.ds(y, padded, stride=cells), :]
        odd = tiles[pl.ds(y + 1, padded, stride=cells), :]
        where = slice(y * cells, y * cells + lanes)
        real = jnp.where(low, even, pltpu.roll(odd, cells, 1))
        imag = jnp.where(low, pltpu.roll(even, cells, 1), odd)
        lined[:, where] = jnp.concatenate([real, imag], axis=0).astype(BF16)
    best = None
    wide = 8 * lanes
    for block in range(cells * cells // wide):
        scores = jnp.dot(
            x_back[...], lined[:, block * wide : (block + 1) * wide], preferred_element_type=F32
        )
        for piece in range(wide // lanes):
            part = scores[:, piece * lanes : (piece + 1) * lanes]
            best = part if best is None else jnp.maximum(best, part)
    top = jnp.max(best, axis=1, keepdims=True) * (1.0 / (cells * math.sqrt(cells)))
    out[...] = jnp.broadcast_to(top, (cells, lanes))


def inverse(core, weights, receptor, first, second, arrived, tables, padded):
    mine, half, cells, lanes = receptor.shape
    best = pl.pallas_call(
        lambda *refs: inverse_kernel(padded, *refs),
        out_shape=jax.ShapeDtypeStruct((cells, lanes), F32),
        in_specs=[smem(), smem()] + [vmem()] * 7,
        out_specs=vmem(),
        scratch_shapes=[
            pltpu.VMEM((padded * cells, lanes), F32),
            pltpu.VMEM((2 * padded, cells * cells), BF16),
        ],
        name="inverse_pair",
        cost_estimate=pl.CostEstimate(
            flops=half * 6 * lanes * lanes * cells,
            bytes_accessed=half * cells * lanes * 16,
            transcendentals=0,
        ),
    )(core, weights, receptor, first, second, arrived, *tables)
    return best[:, 0]


def shards(receptor_occupancy, ligand_occupancy, rot_index, receptor_extent, channel_weight):
    channels = receptor_occupancy.shape[1]
    thickness = receptor_occupancy.shape[2]
    parts = lax.axis_size("fft")
    if parts != LIG_STEPS or channels % parts:
        raise ValueError("unsupported split")
    mine = channels // parts
    cells = thickness * parts
    half = cells // 2 + 1
    padded = -(-half // 8) * 8
    me = lax.axis_index("fft").astype(jnp.int32)
    forward_tables, backward_tables = make_tables(cells, half, padded)
    turns = rot_index[0]
    zero = jnp.zeros((), jnp.int32)
    receptor_sel = jnp.stack([me, zero, zero, zero])
    ligand_sel = jnp.stack(
        [
            me,
            ((turns == 1) | (turns == 2)).astype(jnp.int32),
            (turns >= 2).astype(jnp.int32),
            turns % 2,
        ]
    )

    def other_channels(occupancy):
        theirs = lax.dynamic_slice_in_dim(occupancy[0], (1 - me) * mine, mine, 0)
        return passed_along(theirs.astype(BF16), "fft", 1)

    extents = [receptor_extent]
    for _ in range(REC_STEPS - 1):
        extents.append(passed_along(extents[-1], "rec", 1))
    receptor_in = other_channels(receptor_occupancy)
    ligand_in = other_channels(ligand_occupancy)
    receptor = forward(
        receptor_occupancy, receptor_in, receptor_sel, forward_tables, half, padded
    )
    receptors = [receptor]
    for _ in range(REC_STEPS - 1):
        receptors.append(passed_along(receptors[-1], "rec", 1))
    first = forward(ligand_occupancy, ligand_in, ligand_sel, forward_tables, half, padded)
    second = passed_along(first, "lig", 1)
    weights = channel_weight * (1.0 / float(cells) ** 3)
    core = me[None]
    tops = []
    for step in range(REC_STEPS):
        sent = send_part(core, weights, receptors[step], first, second)
        arrived = passed_along(sent, "fft", 1)
        tops.append(
            inverse(core, weights, receptors[step], first, second, arrived, backward_tables, padded)
        )
    tops = jnp.stack(tops).reshape(REC_STEPS, parts, thickness)
    theirs = passed_along(lax.dynamic_index_in_dim(tops, 1 - me, 1, False), "fft", 1)
    ours = lax.dynamic_index_in_dim(tops, me, 1, False)
    steps = jnp.arange(LIG_STEPS, dtype=jnp.int32)[None, :, None]
    both = jnp.where(steps == me, ours[:, None], theirs[:, None])
    planes = me * thickness + jnp.arange(thickness, dtype=jnp.int32)
    limit = jnp.concatenate(extents)[:, None, None]
    return jnp.where(planes[None, None, :] < limit, both, 0.0)[None]


def solution(mesh):
    placed = (
        P(("groups", "rec", "lig"), None, "fft", None),
        P(("groups", "rec", "lig"), None, "fft", None),
        P(("groups", "rec", "lig")),
        P(("groups", "rec", "lig")),
        P(),
    )
    return jax.shard_map(
        shards,
        mesh=mesh,
        in_specs=placed,
        out_specs=P(("groups", "rec", "lig"), None, None, "fft"),
        check_vma=False,
    )
```

```python
import math

import jax
import jax.numpy as jnp
import numpy as np
from jax import lax
from jax.experimental import pallas as pl
from jax.experimental.pallas import tpu as pltpu
from jax.sharding import PartitionSpec as P

REC_STEPS = 3
LIG_STEPS = 2
F32 = jnp.float32
BF16 = jnp.bfloat16
VMEM_BYTES = 20 * 1024 * 1024


def passed_along(value, axis, steps):
    count = lax.axis_size(axis)
    pairs = [(source, (source + steps) % count) for source in range(count)]
    return lax.ppermute(value, axis, pairs)


def trig_tables(cells):
    indices = np.arange(cells)
    phases = indices[:, None] * indices[None, :] % cells
    angles = phases.astype(np.float32) * np.float32(2.0 * math.pi / cells)
    return np.cos(angles), np.sin(angles)


def lane_mixes(real, imag):
    first = np.block([[real, imag], [-imag, real]])
    second = np.block([[-imag, real], [-real, -imag]])
    return np.concatenate([first, second], axis=0)


def make_tables(cells, half, padded):
    cosine, sine = trig_tables(cells)
    split = cells // 2
    x_rows = np.zeros((2 * padded, cells), np.float32)
    x_rows[:half] = cosine[:half]
    x_rows[padded : padded + half] = -sine[:half]
    x_swapped = np.concatenate([x_rows[:, split:], x_rows[:, :split]], axis=1)
    y_rows = np.concatenate([cosine, -sine], axis=0)
    forward = (
        np.stack([x_rows, x_swapped]),
        np.stack([y_rows, y_rows[:, ::-1]]),
        np.stack([lane_mixes(cosine, -sine), lane_mixes(cosine[::-1], -sine[::-1])]),
    )
    twice = np.full((half,), 2.0, np.float32)
    twice[0] = 1.0
    twice[-1] = 1.0
    x_back = np.zeros((cells, 2 * padded), np.float32)
    x_back[:, :half] = cosine[:, :half] * twice
    x_back[:, padded : padded + half] = -sine[:, :half] * twice
    backward = (
        x_back,
        np.concatenate([cosine, sine], axis=0),
        lane_mixes(cosine, sine),
    )
    return (
        tuple(jnp.asarray(table, BF16) for table in forward),
        tuple(jnp.asarray(table, BF16) for table in backward),
    )


def group_of(half):
    return max(size for size in range(1, 12) if half % size == 0)


def plane_transform(tiles, y_rows, mixes):
    cells, lanes = tiles[0].shape
    mixed = jnp.dot(y_rows, jnp.concatenate(tiles, axis=1), preferred_element_type=F32)
    mixed = mixed.astype(BF16)
    parts = [mixed[:, n * lanes : (n + 1) * lanes] for n in range(len(tiles))]
    real = jnp.concatenate([part[:cells] for part in parts], axis=0)
    imag = jnp.concatenate([part[cells:] for part in parts], axis=0)
    return jnp.dot(
        jnp.concatenate([real, imag], axis=1), mixes, preferred_element_type=F32
    )


def forward_kernel(
    half, padded, rotated, core, turns, own, received, x_rows, y_rows, mixes, *refs
):
    out, tiles = refs[-2:]
    cells = y_rows.shape[2]
    lanes = 2 * cells
    group = group_of(half)
    grid = jnp.concatenate([own[0, 0].astype(F32).astype(BF16), received[0]], axis=0)
    low = lax.broadcasted_iota(jnp.int32, (padded, lanes), 1) < cells
    wide = 8 * lanes
    for block in range(cells * cells // wide):
        rows = jnp.dot(
            x_rows[0], grid[:, block * wide : (block + 1) * wide], preferred_element_type=F32
        )
        for piece in range(wide // lanes):
            real = rows[:padded, piece * lanes : (piece + 1) * lanes]
            imag = rows[padded:, piece * lanes : (piece + 1) * lanes]
            y = 2 * (block * (wide // lanes) + piece)
            tiles[pl.ds(y, padded, stride=cells), :] = jnp.where(
                low, real, pltpu.roll(imag, cells, 1)
            )
            tiles[pl.ds(y + 1, padded, stride=cells), :] = jnp.where(
                low, pltpu.roll(real, cells, 1), imag
            )

    def tile_at(k):
        return pl.ds(pl.multiple_of(k * cells, cells), cells)

    if rotated:

        @pl.when(turns[0] % 2 == 1)
        def _():
            def turn(step, carry):
                for n in range(group):
                    where = tile_at(step * group + n)
                    turned = jnp.transpose(tiles[where, :])
                    tiles[where, :] = jnp.concatenate([turned[:cells], turned[cells:]], axis=1)
                return carry

            lax.fori_loop(0, half // group, turn, 0)

    def body(step, carry):
        loaded = [tiles[tile_at(step * group + n), :].astype(BF16) for n in range(group)]
        done = plane_transform(loaded, y_rows[0], mixes[0])
        out[pl.ds(step * group, group)] = done.astype(BF16).reshape(group, cells, lanes)
        return carry

    lax.fori_loop(0, half // group, body, 0)


def forward(occupancy, received, core, turns, tables, half, padded, rotated, channel, after):
    mine, thickness, plane = received.shape
    cells = tables[1].shape[2]
    lanes = 2 * cells

    def y_reversed(turns):
        return (((turns[0] + 1) % 4) // 2 if rotated else 0, 0, 0)

    def z_reversed(turns):
        return (turns[0] // 2 if rotated else 0, 0, 0)

    grid_spec = pltpu.PrefetchScalarGridSpec(
        num_scalar_prefetch=2,
        grid=(1,),
        in_specs=[
            pl.BlockSpec((1, 1, thickness, plane), lambda c, f, t: (0, f[0] * mine + channel, 0, 0)),
            pl.BlockSpec((1, thickness, plane), lambda c, f, t: (channel, 0, 0)),
            pl.BlockSpec((1, 2 * padded, cells), lambda c, f, t: (f[0], 0, 0)),
            pl.BlockSpec((1, lanes, cells), lambda c, f, t: y_reversed(t)),
            pl.BlockSpec((1, 2 * lanes, lanes), lambda c, f, t: z_reversed(t)),
        ]
        + [pl.BlockSpec(memory_space=pl.ANY)] * len(after),
        out_specs=pl.BlockSpec((half, cells, lanes), lambda c, f, t: (0, 0, 0)),
        scratch_shapes=[pltpu.VMEM((padded * cells, lanes), F32)],
    )
    return pl.pallas_call(
        lambda *refs: forward_kernel(half, padded, rotated, *refs),
        out_shape=jax.ShapeDtypeStruct((half, cells, lanes), BF16),
        grid_spec=grid_spec,
        name="forward_pose" if rotated else "forward_receptor",
        compiler_params=pltpu.CompilerParams(vmem_limit_bytes=VMEM_BYTES),
        cost_estimate=pl.CostEstimate(
            flops=half * 6 * lanes * lanes * cells,
            bytes_accessed=plane * thickness * 20,
            transcendentals=0,
        ),
    )(core, turns, occupancy, received, *tables, *after)


def partial_cross(scales, receptors, ligands, where, cells):
    same = None
    swapped = None
    for scale, receptor, ligand in zip(scales, receptors, ligands):
        left = receptor[where].astype(F32) * scale
        right = ligand(where).astype(F32)
        turned = pltpu.roll(right, cells, right.ndim - 1)
        same = left * right if same is None else same + left * right
        swapped = left * turned if swapped is None else swapped + left * turned
    axis = same.ndim - 1
    low = lax.broadcasted_iota(jnp.int32, same.shape, axis) < cells
    real = same + pltpu.roll(same, cells, axis)
    imag = swapped - pltpu.roll(swapped, cells, axis)
    return jnp.where(low, real, imag)


def chosen(pick_second, first, second):
    return lambda where: jnp.where(pick_second, second[where], first[where])


def cross_kernel(mine, keep, core, weights, *refs):
    receptors, firsts, seconds = refs[:mine], refs[mine : 2 * mine], refs[2 * mine : 3 * mine]
    out = refs[-1]
    half, cells, lanes = out.shape
    group = group_of(half)
    volume = 1.0 / float(cells) ** 3
    scales = [weights[core[0] * mine + c] * volume for c in range(mine)]
    second = core[0] == (1 if keep else 0)
    ligands = [chosen(second, *pair) for pair in zip(firsts, seconds)]

    def body(step, carry):
        for n in range(group):
            k = step * group + n
            out[k] = partial_cross(scales, receptors, ligands, k, cells).astype(out.dtype)
        return carry

    lax.fori_loop(0, half // group, body, 0)


def vmem():
    return pl.BlockSpec(memory_space=pltpu.VMEM)


def smem():
    return pl.BlockSpec(memory_space=pltpu.SMEM)


def cross_part(keep, core, weights, receptor, first, second, after):
    mine = len(receptor)
    half, cells, lanes = receptor[0].shape
    return pl.pallas_call(
        lambda *refs: cross_kernel(mine, keep, *refs),
        out_shape=jax.ShapeDtypeStruct((half, cells, lanes), F32 if keep else BF16),
        in_specs=[smem(), smem()]
        + [vmem()] * (3 * mine)
        + [pl.BlockSpec(memory_space=pl.ANY)] * len(after),
        out_specs=vmem(),
        name="cross_keep" if keep else "cross_send",
        compiler_params=pltpu.CompilerParams(vmem_limit_bytes=VMEM_BYTES),
        cost_estimate=pl.CostEstimate(
            flops=mine * half * cells * lanes * 10,
            bytes_accessed=half * cells * lanes * 14,
            transcendentals=0,
        ),
    )(core, weights, *receptor, *first, *second, *after)


def inverse_kernel(padded, kept, arrived, x_back, y_rows, mixes, *refs):
    out, tiles, lined = refs[-3:]
    half, cells, lanes = kept.shape
    group = group_of(half)
    tiles[half * cells :, :] = jnp.zeros(((padded - half) * cells, lanes), F32)
    row = lax.broadcasted_iota(jnp.int32, (cells, lanes), 0)
    lane = lax.broadcasted_iota(jnp.int32, (cells, lanes), 1) % cells
    origin = row + lane

    def body(step, carry):
        loaded = []
        for n in range(group):
            k = step * group + n
            cross = kept[k] + arrived[k].astype(F32)
            if n == 0:
                cross = jnp.where(origin + k > 0, cross, 0.0)
            loaded.append(cross.astype(BF16))
        done = plane_transform(loaded, y_rows[...], mixes[...])
        size = group * cells
        tiles[pl.ds(pl.multiple_of(step * size, size), size), :] = done
        return carry

    lax.fori_loop(0, half // group, body, 0)
    low = lax.broadcasted_iota(jnp.int32, (padded, lanes), 1) < cells
    for y in range(0, cells, 2):
        even = tiles[pl.ds(y, padded, stride=cells), :]
        odd = tiles[pl.ds(y + 1, padded, stride=cells), :]
        where = slice(y * cells, y * cells + lanes)
        real = jnp.where(low, even, pltpu.roll(odd, cells, 1))
        imag = jnp.where(low, pltpu.roll(even, cells, 1), odd)
        lined[:, where] = jnp.concatenate([real, imag], axis=0).astype(BF16)
    best = None
    wide = 8 * lanes
    for block in range(cells * cells // wide):
        scores = jnp.dot(
            x_back[...], lined[:, block * wide : (block + 1) * wide], preferred_element_type=F32
        )
        for piece in range(wide // lanes):
            part = scores[:, piece * lanes : (piece + 1) * lanes]
            best = part if best is None else jnp.maximum(best, part)
    top = jnp.max(jnp.transpose(best), axis=0, keepdims=True)
    out[...] = top * (1.0 / (cells * math.sqrt(cells)))


def inverse(kept, arrived, tables, padded, after):
    half, cells, lanes = kept.shape
    return pl.pallas_call(
        lambda *refs: inverse_kernel(padded, *refs),
        out_shape=jax.ShapeDtypeStruct((1, cells), F32),
        in_specs=[vmem()] * 5 + [pl.BlockSpec(memory_space=pl.ANY)] * len(after),
        out_specs=vmem(),
        scratch_shapes=[
            pltpu.VMEM((padded * cells, lanes), F32),
            pltpu.VMEM((2 * padded, cells * cells), BF16),
        ],
        name="inverse_pair",
        compiler_params=pltpu.CompilerParams(vmem_limit_bytes=VMEM_BYTES),
        cost_estimate=pl.CostEstimate(
            flops=half * 6 * lanes * lanes * cells,
            bytes_accessed=half * cells * lanes * 16,
            transcendentals=0,
        ),
    )(kept, arrived, *tables, *after)


def shards(receptor_occupancy, ligand_occupancy, rot_index, receptor_extent, channel_weight):
    channels = receptor_occupancy.shape[1]
    thickness = receptor_occupancy.shape[2]
    parts = lax.axis_size("fft")
    if parts != LIG_STEPS or channels % parts:
        raise ValueError("unsupported split")
    mine = channels // parts
    cells = thickness * parts
    half = cells // 2 + 1
    padded = -(-half // 8) * 8
    me = lax.axis_index("fft").astype(jnp.int32)
    forward_tables, backward_tables = make_tables(cells, half, padded)
    core = me[None]

    def other_channels(occupancy):
        theirs = lax.dynamic_slice_in_dim(occupancy[0], (1 - me) * mine, mine, 0)
        return passed_along(theirs.astype(BF16), "fft", 1)

    extents = [receptor_extent]
    for _ in range(REC_STEPS - 1):
        extents.append(passed_along(extents[-1], "rec", 1))
    receptor_in = other_channels(receptor_occupancy)
    ligand_in = other_channels(ligand_occupancy)
    def spectra(occupancy, received, rotated, after):
        done = []
        for channel in range(mine):
            spectrum = forward(
                occupancy, received, core, rot_index, forward_tables, half, padded, rotated,
                channel, (done or after)[-1:],
            )
            done.append(spectrum)
        return done

    receptors = [spectra(receptor_occupancy, receptor_in, False, [])]
    for _ in range(REC_STEPS - 1):
        receptors.append([passed_along(spectrum, "rec", 1) for spectrum in receptors[-1]])
    first = spectra(ligand_occupancy, ligand_in, True, receptors[0])
    second = [passed_along(spectrum, "lig", 1) for spectrum in first]

    def crossed(keep, step, after):
        return cross_part(keep, core, channel_weight, receptors[step], first, second, after)

    tops = [None] * REC_STEPS
    pending = []
    last = []
    for step in (1, 0, *range(2, REC_STEPS)):
        sent = crossed(False, step, last)
        arrived = passed_along(sent, "fft", 1)
        kept = crossed(True, step, [sent])
        pending.append((step, kept, arrived))
        last = [kept]
        if step == 1:
            continue
        while pending:
            place, kept, arrived = pending.pop(0)
            tops[place] = inverse(kept, arrived, backward_tables, padded, last)
            last = [tops[place]]
    ours = jnp.concatenate(tops, axis=0)
    theirs = passed_along(ours, "fft", 1)
    start = me * thickness
    ours = lax.dynamic_slice_in_dim(ours, start, thickness, 1)
    theirs = lax.dynamic_slice_in_dim(theirs, start, thickness, 1)
    steps = jnp.arange(LIG_STEPS, dtype=jnp.int32)[None, :, None]
    both = jnp.where(steps == me, ours[:, None], theirs[:, None])
    planes = start + jnp.arange(thickness, dtype=jnp.int32)
    limit = jnp.concatenate(extents)[:, None, None]
    return jnp.where(planes[None, None, :] < limit, both, 0.0)[None]


def solution(mesh):
    placed = (
        P(("groups", "rec", "lig"), None, "fft", None),
        P(("groups", "rec", "lig"), None, "fft", None),
        P(("groups", "rec", "lig")),
        P(("groups", "rec", "lig")),
        P(),
    )
    return jax.shard_map(
        shards,
        mesh=mesh,
        in_specs=placed,
        out_specs=P(("groups", "rec", "lig"), None, None, "fft"),
        check_vma=False,
    )
```

```python
import math

import jax
import jax.numpy as jnp
import numpy as np
from jax import lax
from jax.experimental import pallas as pl
from jax.experimental.pallas import tpu as pltpu
from jax.sharding import PartitionSpec as P


REC_STEPS = 3
LIG_STEPS = 2
F32 = jnp.float32
BF16 = jnp.bfloat16
VMEM_BYTES = 20 * 1024 * 1024


def passed_along(value, axis, steps):
    count = lax.axis_size(axis)
    pairs = [(source, (source + steps) % count) for source in range(count)]
    return lax.ppermute(value, axis, pairs)


def trig_tables(cells):
    indices = np.arange(cells)
    phases = indices[:, None] * indices[None, :] % cells
    angles = phases.astype(np.float32) * np.float32(2.0 * math.pi / cells)
    return np.cos(angles), np.sin(angles)


def lane_mixes(real, imag):
    first = np.block([[real, imag], [-imag, real]])
    second = np.block([[-imag, real], [-real, -imag]])
    return np.concatenate([first, second], axis=0)


def make_tables(cells, half, padded):
    cosine, sine = trig_tables(cells)
    split = cells // 2
    x_rows = np.zeros((2 * padded, cells), np.float32)
    x_rows[:half] = cosine[:half]
    x_rows[padded : padded + half] = -sine[:half]
    x_swapped = np.concatenate([x_rows[:, split:], x_rows[:, :split]], axis=1)
    y_rows = np.concatenate([cosine, -sine], axis=0)
    forward = (
        np.stack([x_rows, x_swapped]),
        np.stack([y_rows, y_rows[:, ::-1]]),
        np.stack([lane_mixes(cosine, -sine), lane_mixes(cosine[::-1], -sine[::-1])]),
    )
    twice = np.full((half,), 2.0, np.float32)
    twice[0] = 1.0
    twice[-1] = 1.0
    x_back = np.zeros((cells, 2 * padded), np.float32)
    x_back[:, :half] = cosine[:, :half] * twice
    x_back[:, padded : padded + half] = -sine[:, :half] * twice
    backward = (
        x_back,
        np.concatenate([cosine, sine], axis=0),
        lane_mixes(cosine, sine),
    )
    return (
        tuple(jnp.asarray(table, BF16) for table in forward),
        tuple(jnp.asarray(table, BF16) for table in backward),
    )


def group_of(half):
    return max(size for size in range(1, 12) if half % size == 0)


def plane_transform(tiles, y_rows, mixes):
    cells, lanes = tiles[0].shape
    mixed = jnp.dot(y_rows, jnp.concatenate(tiles, axis=1), preferred_element_type=F32)
    mixed = mixed.astype(BF16)
    parts = [mixed[:, n * lanes : (n + 1) * lanes] for n in range(len(tiles))]
    real = jnp.concatenate([part[:cells] for part in parts], axis=0)
    imag = jnp.concatenate([part[cells:] for part in parts], axis=0)
    return jnp.dot(
        jnp.concatenate([real, imag], axis=1), mixes, preferred_element_type=F32
    )


def forward_kernel(
    half, padded, rotated, core, turns, own, received, x_rows, y_rows, mixes, *refs
):
    out, tiles = refs[-2:]
    cells = y_rows.shape[2]
    lanes = 2 * cells
    group = group_of(half)
    grid = jnp.concatenate([own[0, 0].astype(F32).astype(BF16), received[0]], axis=0)
    low = lax.broadcasted_iota(jnp.int32, (padded, lanes), 1) < cells
    wide = 8 * lanes
    for block in range(cells * cells // wide):
        rows = jnp.dot(
            x_rows[0], grid[:, block * wide : (block + 1) * wide], preferred_element_type=F32
        )
        for piece in range(wide // lanes):
            real = rows[:padded, piece * lanes : (piece + 1) * lanes]
            imag = rows[padded:, piece * lanes : (piece + 1) * lanes]
            y = 2 * (block * (wide // lanes) + piece)
            tiles[pl.ds(y, padded, stride=cells), :] = jnp.where(
                low, real, pltpu.roll(imag, cells, 1)
            )
            tiles[pl.ds(y + 1, padded, stride=cells), :] = jnp.where(
                low, pltpu.roll(real, cells, 1), imag
            )

    def tile_at(k):
        return pl.ds(pl.multiple_of(k * cells, cells), cells)

    if rotated:

        @pl.when(turns[0] % 2 == 1)
        def _():
            def turn(step, carry):
                for n in range(group):
                    where = tile_at(step * group + n)
                    turned = jnp.transpose(tiles[where, :])
                    tiles[where, :] = jnp.concatenate([turned[:cells], turned[cells:]], axis=1)
                return carry

            lax.fori_loop(0, half // group, turn, 0)

    def body(step, carry):
        loaded = [tiles[tile_at(step * group + n), :].astype(BF16) for n in range(group)]
        done = plane_transform(loaded, y_rows[0], mixes[0])
        out[pl.ds(step * group, group)] = done.astype(BF16).reshape(group, cells, lanes)
        return carry

    lax.fori_loop(0, half // group, body, 0)


def forward(occupancy, received, core, turns, tables, half, padded, rotated, channel, after):
    mine, thickness, plane = received.shape
    cells = tables[1].shape[2]
    lanes = 2 * cells

    def y_reversed(turns):
        return (((turns[0] + 1) % 4) // 2 if rotated else 0, 0, 0)

    def z_reversed(turns):
        return (turns[0] // 2 if rotated else 0, 0, 0)

    grid_spec = pltpu.PrefetchScalarGridSpec(
        num_scalar_prefetch=2,
        grid=(1,),
        in_specs=[
            pl.BlockSpec((1, 1, thickness, plane), lambda c, f, t: (0, f[0] * mine + channel, 0, 0)),
            pl.BlockSpec((1, thickness, plane), lambda c, f, t: (channel, 0, 0)),
            pl.BlockSpec((1, 2 * padded, cells), lambda c, f, t: (f[0], 0, 0)),
            pl.BlockSpec((1, lanes, cells), lambda c, f, t: y_reversed(t)),
            pl.BlockSpec((1, 2 * lanes, lanes), lambda c, f, t: z_reversed(t)),
        ]
        + [pl.BlockSpec(memory_space=pl.ANY)] * len(after),
        out_specs=pl.BlockSpec((half, cells, lanes), lambda c, f, t: (0, 0, 0)),
        scratch_shapes=[pltpu.VMEM((padded * cells, lanes), F32)],
    )
    return pl.pallas_call(
        lambda *refs: forward_kernel(half, padded, rotated, *refs),
        out_shape=jax.ShapeDtypeStruct((half, cells, lanes), BF16),
        grid_spec=grid_spec,
        name="forward_pose" if rotated else "forward_receptor",
        compiler_params=pltpu.CompilerParams(vmem_limit_bytes=VMEM_BYTES),
        cost_estimate=pl.CostEstimate(
            flops=half * 6 * lanes * lanes * cells,
            bytes_accessed=plane * thickness * 20,
            transcendentals=0,
        ),
    )(core, turns, occupancy, received, *tables, *after)


def partial_cross(scales, receptors, ligands, where, cells):
    same = None
    swapped = None
    for scale, receptor, ligand in zip(scales, receptors, ligands):
        left = receptor[where].astype(F32) * scale
        right = ligand(where).astype(F32)
        turned = pltpu.roll(right, cells, right.ndim - 1)
        same = left * right if same is None else same + left * right
        swapped = left * turned if swapped is None else swapped + left * turned
    axis = same.ndim - 1
    low = lax.broadcasted_iota(jnp.int32, same.shape, axis) < cells
    real = same + pltpu.roll(same, cells, axis)
    imag = swapped - pltpu.roll(swapped, cells, axis)
    return jnp.where(low, real, imag)


def chosen(pick_second, first, second):
    return lambda where: jnp.where(pick_second, second[where], first[where])


def cross_kernel(mine, keep, core, weights, *refs):
    receptors, firsts, seconds = refs[:mine], refs[mine : 2 * mine], refs[2 * mine : 3 * mine]
    out = refs[-1]
    group, cells, _ = out.shape
    volume = 1.0 / float(cells) ** 3
    scales = [weights[core[0] * mine + c] * volume for c in range(mine)]
    second = core[0] == int(keep)
    ligands = [chosen(second, *pair) for pair in zip(firsts, seconds)]

    for k in range(group):
        out[k] = partial_cross(scales, receptors, ligands, k, cells).astype(out.dtype)


def vmem():
    return pl.BlockSpec(memory_space=pltpu.VMEM)


def smem():
    return pl.BlockSpec(memory_space=pltpu.SMEM)


def cross_part(keep, core, weights, receptor, first, second, after):
    mine = len(receptor)
    half, cells, lanes = receptor[0].shape
    group = group_of(half)
    block = (group, cells, lanes)

    def used(is_second):
        def index(k, core):
            wanted = int(keep) if is_second else int(not keep)
            return (jnp.where(core[0] == wanted, k, 0), 0, 0)

        return pl.BlockSpec(block, index)

    grid_spec = pltpu.PrefetchScalarGridSpec(
        num_scalar_prefetch=1,
        grid=(half // group,),
        in_specs=[smem()]
        + [pl.BlockSpec(block, lambda k, core: (k, 0, 0))] * mine
        + [used(False)] * mine
        + [used(True)] * mine
        + [pl.BlockSpec(memory_space=pl.ANY)] * len(after),
        out_specs=pl.BlockSpec(block, lambda k, core: (k, 0, 0)),
    )
    return pl.pallas_call(
        lambda *refs: cross_kernel(mine, keep, *refs),
        out_shape=jax.ShapeDtypeStruct((half, cells, lanes), F32 if keep else BF16),
        grid_spec=grid_spec,
        name="cross_keep" if keep else "cross_send",
        compiler_params=pltpu.CompilerParams(vmem_limit_bytes=VMEM_BYTES),
        cost_estimate=pl.CostEstimate(
            flops=mine * half * cells * lanes * 10,
            bytes_accessed=half * cells * lanes * 14,
            transcendentals=0,
        ),
    )(core, weights, *receptor, *first, *second, *after)


def inverse_kernel(padded, kept, arrived, x_back, y_rows, mixes, *refs):
    out, tiles, lined = refs[-3:]
    half, cells, lanes = kept.shape
    group = group_of(half)
    tiles[half * cells :, :] = jnp.zeros(((padded - half) * cells, lanes), F32)
    row = lax.broadcasted_iota(jnp.int32, (cells, lanes), 0)
    lane = lax.broadcasted_iota(jnp.int32, (cells, lanes), 1) % cells
    origin = row + lane

    def body(step, carry):
        loaded = []
        for n in range(group):
            k = step * group + n
            cross = kept[k] + arrived[k].astype(F32)
            if n == 0:
                cross = jnp.where(origin + k > 0, cross, 0.0)
            loaded.append(cross.astype(BF16))
        done = plane_transform(loaded, y_rows[...], mixes[...])
        size = group * cells
        tiles[pl.ds(pl.multiple_of(step * size, size), size), :] = done
        return carry

    lax.fori_loop(0, half // group, body, 0)
    low = lax.broadcasted_iota(jnp.int32, (padded, lanes), 1) < cells
    for y in range(0, cells, 2):
        even = tiles[pl.ds(y, padded, stride=cells), :]
        odd = tiles[pl.ds(y + 1, padded, stride=cells), :]
        where = slice(y * cells, y * cells + lanes)
        real = jnp.where(low, even, pltpu.roll(odd, cells, 1))
        imag = jnp.where(low, pltpu.roll(even, cells, 1), odd)
        lined[:, where] = jnp.concatenate([real, imag], axis=0).astype(BF16)
    best = None
    wide = 8 * lanes
    for block in range(cells * cells // wide):
        scores = jnp.dot(
            x_back[...], lined[:, block * wide : (block + 1) * wide], preferred_element_type=F32
        )
        for piece in range(wide // lanes):
            part = scores[:, piece * lanes : (piece + 1) * lanes]
            best = part if best is None else jnp.maximum(best, part)
    top = jnp.max(jnp.transpose(best), axis=0, keepdims=True)
    out[...] = top * (1.0 / (cells * math.sqrt(cells)))


def inverse(kept, arrived, tables, padded, after):
    half, cells, lanes = kept.shape
    return pl.pallas_call(
        lambda *refs: inverse_kernel(padded, *refs),
        out_shape=jax.ShapeDtypeStruct((1, cells), F32),
        in_specs=[vmem()] * 5 + [pl.BlockSpec(memory_space=pl.ANY)] * len(after),
        out_specs=vmem(),
        scratch_shapes=[
            pltpu.VMEM((padded * cells, lanes), F32),
            pltpu.VMEM((2 * padded, cells * cells), BF16),
        ],
        name="inverse_pair",
        compiler_params=pltpu.CompilerParams(vmem_limit_bytes=VMEM_BYTES),
        cost_estimate=pl.CostEstimate(
            flops=half * 6 * lanes * lanes * cells,
            bytes_accessed=half * cells * lanes * 16,
            transcendentals=0,
        ),
    )(kept, arrived, *tables, *after)


def shards(receptor_occupancy, ligand_occupancy, rot_index, receptor_extent, channel_weight):
    channels = receptor_occupancy.shape[1]
    thickness = receptor_occupancy.shape[2]
    parts = lax.axis_size("fft")
    if parts != LIG_STEPS or channels % parts:
        raise ValueError("unsupported split")
    mine = channels // parts
    cells = thickness * parts
    half = cells // 2 + 1
    padded = -(-half // 8) * 8
    me = lax.axis_index("fft").astype(jnp.int32)
    forward_tables, backward_tables = make_tables(cells, half, padded)
    core = me[None]

    def other_channels(occupancy):
        theirs = lax.dynamic_slice_in_dim(occupancy[0], (1 - me) * mine, mine, 0)
        return passed_along(theirs.astype(BF16), "fft", 1)

    extents = [receptor_extent]
    for steps in range(1, REC_STEPS):
        extents.append(passed_along(receptor_extent, "rec", steps))
    receptor_in = other_channels(receptor_occupancy)
    ligand_in = other_channels(ligand_occupancy)

    def hopped(value, axis):
        return passed_along(value, axis, 1)

    def spectrum(rotated, channel, after):
        occupancy, received = (
            (ligand_occupancy, ligand_in) if rotated else (receptor_occupancy, receptor_in)
        )
        return forward(
            occupancy, received, core, rot_index, forward_tables, half, padded, rotated,
            channel, after,
        )

    receptor = [spectrum(False, 0, [])]
    first = []
    for channel in range(mine):
        first.append(spectrum(True, channel, [*receptor, *first][-1:]))
    for channel in range(1, mine):
        receptor.append(spectrum(False, channel, [*first, *receptor[1:]][-1:]))
    receptors = [receptor]
    for _ in range(1, REC_STEPS):
        receptors.append([hopped(each, "rec") for each in receptors[-1]])
    second = [hopped(each, "lig") for each in first]

    def crossed(keep, step, after):
        return cross_part(keep, core, channel_weight, receptors[step], first, second, after)

    tops = [None] * REC_STEPS
    pending = []
    last = []
    for step in (1, 0, *range(2, REC_STEPS)):
        sent = crossed(False, step, last)
        arrived = passed_along(sent, "fft", 1)
        kept = crossed(True, step, [sent])
        pending.append((step, kept, arrived))
        last = [kept]
        if step == 1:
            continue
        while pending:
            place, kept, arrived = pending.pop(0)
            tops[place] = inverse(kept, arrived, backward_tables, padded, last)
            last = [tops[place]]
    ours = jnp.concatenate(tops, axis=0)
    theirs = passed_along(ours, "fft", 1)
    start = me * thickness
    ours = lax.dynamic_slice_in_dim(ours, start, thickness, 1)
    theirs = lax.dynamic_slice_in_dim(theirs, start, thickness, 1)
    steps = jnp.arange(LIG_STEPS, dtype=jnp.int32)[None, :, None]
    both = jnp.where(steps == me, ours[:, None], theirs[:, None])
    planes = start + jnp.arange(thickness, dtype=jnp.int32)
    limit = jnp.concatenate(extents)[:, None, None]
    return jnp.where(planes[None, None, :] < limit, both, 0.0)[None]


def solution(mesh):
    placed = (
        P(("groups", "rec", "lig"), None, "fft", None),
        P(("groups", "rec", "lig"), None, "fft", None),
        P(("groups", "rec", "lig")),
        P(("groups", "rec", "lig")),
        P(),
    )

    return jax.shard_map(
        shards,
        mesh=mesh,
        in_specs=placed,
        out_specs=P(("groups", "rec", "lig"), None, None, "fft"),
        check_vma=False,
    )
```

```python
import math

import jax
import jax.numpy as jnp
import numpy as np
from jax import lax
from jax.experimental import pallas as pl
from jax.experimental.pallas import tpu as pltpu
from jax.sharding import PartitionSpec as P


REC_STEPS = 3
LIG_STEPS = 2
F32 = jnp.float32
BF16 = jnp.bfloat16
VMEM_BYTES = 20 * 1024 * 1024


def passed_along(value, axis, steps):
    count = lax.axis_size(axis)
    pairs = [(source, (source + steps) % count) for source in range(count)]
    return lax.ppermute(value, axis, pairs)


def trig_tables(cells):
    indices = np.arange(cells)
    phases = indices[:, None] * indices[None, :] % cells
    angles = phases.astype(np.float32) * np.float32(2.0 * math.pi / cells)
    return np.cos(angles), np.sin(angles)


def lane_mixes(real, imag):
    first = np.block([[real, imag], [-imag, real]])
    second = np.block([[-imag, real], [-real, -imag]])
    return np.concatenate([first, second], axis=0)


def make_tables(cells, half, padded):
    cosine, sine = trig_tables(cells)
    split = cells // 2
    x_rows = np.zeros((2 * padded, cells), np.float32)
    x_rows[:half] = cosine[:half]
    x_rows[padded : padded + half] = -sine[:half]
    x_swapped = np.concatenate([x_rows[:, split:], x_rows[:, :split]], axis=1)
    y_rows = np.concatenate([cosine, -sine], axis=0)
    forward = (
        np.stack([x_rows, x_swapped]),
        np.stack([y_rows, y_rows[:, ::-1]]),
        np.stack([lane_mixes(cosine, -sine), lane_mixes(cosine[::-1], -sine[::-1])]),
    )
    twice = np.full((half,), 2.0, np.float32)
    twice[0] = 1.0
    twice[-1] = 1.0
    x_back = np.zeros((cells, 2 * padded), np.float32)
    x_back[:, :half] = cosine[:, :half] * twice
    x_back[:, padded : padded + half] = -sine[:, :half] * twice
    backward = (
        x_back,
        np.concatenate([cosine, sine], axis=0),
        lane_mixes(cosine, sine),
    )
    return (
        tuple(jnp.asarray(table, BF16) for table in forward),
        tuple(jnp.asarray(table, BF16) for table in backward),
    )


def group_of(half):
    return max(size for size in range(1, 12) if half % size == 0)


def plane_transform(tiles, y_rows, mixes):
    cells, lanes = tiles[0].shape
    mixed = jnp.dot(y_rows, jnp.concatenate(tiles, axis=1), preferred_element_type=F32)
    mixed = mixed.astype(BF16)
    parts = [mixed[:, n * lanes : (n + 1) * lanes] for n in range(len(tiles))]
    real = jnp.concatenate([part[:cells] for part in parts], axis=0)
    imag = jnp.concatenate([part[cells:] for part in parts], axis=0)
    return jnp.dot(
        jnp.concatenate([real, imag], axis=1), mixes, preferred_element_type=F32
    )


def forward_kernel(
    half, padded, rotated, core, turns, own, received, x_rows, y_rows, mixes, *refs
):
    out, tiles = refs[-2:]
    cells = y_rows.shape[2]
    lanes = 2 * cells
    group = group_of(half)
    grid = jnp.concatenate([own[0, 0].astype(F32).astype(BF16), received[0]], axis=0)
    low = lax.broadcasted_iota(jnp.int32, (padded, lanes), 1) < cells
    wide = 8 * lanes
    for block in range(cells * cells // wide):
        rows = jnp.dot(
            x_rows[0], grid[:, block * wide : (block + 1) * wide], preferred_element_type=F32
        )
        for piece in range(wide // lanes):
            real = rows[:padded, piece * lanes : (piece + 1) * lanes]
            imag = rows[padded:, piece * lanes : (piece + 1) * lanes]
            y = 2 * (block * (wide // lanes) + piece)
            tiles[pl.ds(y, padded, stride=cells), :] = jnp.where(
                low, real, pltpu.roll(imag, cells, 1)
            )
            tiles[pl.ds(y + 1, padded, stride=cells), :] = jnp.where(
                low, pltpu.roll(real, cells, 1), imag
            )

    def tile_at(k):
        return pl.ds(pl.multiple_of(k * cells, cells), cells)

    if rotated:

        @pl.when(turns[0] % 2 == 1)
        def _():
            def turn(step, carry):
                for n in range(group):
                    where = tile_at(step * group + n)
                    turned = jnp.transpose(tiles[where, :])
                    tiles[where, :] = jnp.concatenate([turned[:cells], turned[cells:]], axis=1)
                return carry

            lax.fori_loop(0, half // group, turn, 0)

    def body(step, carry):
        loaded = [tiles[tile_at(step * group + n), :].astype(BF16) for n in range(group)]
        done = plane_transform(loaded, y_rows[0], mixes[0])
        out[pl.ds(step * group, group)] = done.astype(BF16).reshape(group, cells, lanes)
        return carry

    lax.fori_loop(0, half // group, body, 0)


def forward(occupancy, received, core, turns, tables, half, padded, rotated, channel, after):
    mine, thickness, plane = received.shape
    cells = tables[1].shape[2]
    lanes = 2 * cells

    def y_reversed(turns):
        return (((turns[0] + 1) % 4) // 2 if rotated else 0, 0, 0)

    def z_reversed(turns):
        return (turns[0] // 2 if rotated else 0, 0, 0)

    grid_spec = pltpu.PrefetchScalarGridSpec(
        num_scalar_prefetch=2,
        grid=(1,),
        in_specs=[
            pl.BlockSpec((1, 1, thickness, plane), lambda c, f, t: (0, f[0] * mine + channel, 0, 0)),
            pl.BlockSpec((1, thickness, plane), lambda c, f, t: (channel, 0, 0)),
            pl.BlockSpec((1, 2 * padded, cells), lambda c, f, t: (f[0], 0, 0)),
            pl.BlockSpec((1, lanes, cells), lambda c, f, t: y_reversed(t)),
            pl.BlockSpec((1, 2 * lanes, lanes), lambda c, f, t: z_reversed(t)),
        ]
        + [pl.BlockSpec(memory_space=pl.ANY)] * len(after),
        out_specs=pl.BlockSpec((half, cells, lanes), lambda c, f, t: (0, 0, 0)),
        scratch_shapes=[pltpu.VMEM((padded * cells, lanes), F32)],
    )
    return pl.pallas_call(
        lambda *refs: forward_kernel(half, padded, rotated, *refs),
        out_shape=jax.ShapeDtypeStruct((half, cells, lanes), BF16),
        grid_spec=grid_spec,
        name="forward_pose" if rotated else "forward_receptor",
        compiler_params=pltpu.CompilerParams(vmem_limit_bytes=VMEM_BYTES),
        cost_estimate=pl.CostEstimate(
            flops=half * 6 * lanes * lanes * cells,
            bytes_accessed=plane * thickness * 20,
            transcendentals=0,
        ),
    )(core, turns, occupancy, received, *tables, *after)


def partial_cross(scales, receptors, ligands, where, cells):
    same = None
    swapped = None
    for scale, receptor, ligand in zip(scales, receptors, ligands):
        left = receptor[where].astype(F32) * scale
        right = ligand(where).astype(F32)
        turned = pltpu.roll(right, cells, right.ndim - 1)
        same = left * right if same is None else same + left * right
        swapped = left * turned if swapped is None else swapped + left * turned
    axis = same.ndim - 1
    low = lax.broadcasted_iota(jnp.int32, same.shape, axis) < cells
    real = same + pltpu.roll(same, cells, axis)
    imag = swapped - pltpu.roll(swapped, cells, axis)
    return jnp.where(low, real, imag)


def chosen(pick_second, first, second):
    return lambda where: jnp.where(pick_second, second[where], first[where])


def cross_kernel(mine, keep, core, weights, *refs):
    receptors, firsts, seconds = refs[:mine], refs[mine : 2 * mine], refs[2 * mine : 3 * mine]
    out = refs[-1]
    group, cells, _ = out.shape
    volume = 1.0 / float(cells) ** 3
    scales = [weights[core[0] * mine + c] * volume for c in range(mine)]
    second = core[0] == int(keep)
    ligands = [chosen(second, *pair) for pair in zip(firsts, seconds)]

    for k in range(group):
        out[k] = partial_cross(scales, receptors, ligands, k, cells).astype(out.dtype)


def vmem():
    return pl.BlockSpec(memory_space=pltpu.VMEM)


def smem():
    return pl.BlockSpec(memory_space=pltpu.SMEM)


def cross_part(keep, core, weights, receptor, first, second, after):
    mine = len(receptor)
    half, cells, lanes = receptor[0].shape
    group = group_of(half)
    block = (group, cells, lanes)

    def used(is_second):
        def index(k, core):
            wanted = int(keep) if is_second else int(not keep)
            return (jnp.where(core[0] == wanted, k, 0), 0, 0)

        return pl.BlockSpec(block, index)

    grid_spec = pltpu.PrefetchScalarGridSpec(
        num_scalar_prefetch=1,
        grid=(half // group,),
        in_specs=[smem()]
        + [pl.BlockSpec(block, lambda k, core: (k, 0, 0))] * mine
        + [used(False)] * mine
        + [used(True)] * mine
        + [pl.BlockSpec(memory_space=pl.ANY)] * len(after),
        out_specs=pl.BlockSpec(block, lambda k, core: (k, 0, 0)),
    )
    return pl.pallas_call(
        lambda *refs: cross_kernel(mine, keep, *refs),
        out_shape=jax.ShapeDtypeStruct((half, cells, lanes), F32 if keep else BF16),
        grid_spec=grid_spec,
        name="cross_keep" if keep else "cross_send",
        compiler_params=pltpu.CompilerParams(vmem_limit_bytes=VMEM_BYTES),
        cost_estimate=pl.CostEstimate(
            flops=mine * half * cells * lanes * 10,
            bytes_accessed=half * cells * lanes * 14,
            transcendentals=0,
        ),
    )(core, weights, *receptor, *first, *second, *after)


def inverse_kernel(padded, kept, arrived, x_back, y_rows, mixes, *refs):
    out, tiles, lined = refs[-3:]
    half, cells, lanes = kept.shape
    group = group_of(half)
    tiles[half * cells :, :] = jnp.zeros(((padded - half) * cells, lanes), F32)
    row = lax.broadcasted_iota(jnp.int32, (cells, lanes), 0)
    lane = lax.broadcasted_iota(jnp.int32, (cells, lanes), 1) % cells
    origin = row + lane

    def body(step, carry):
        loaded = []
        for n in range(group):
            k = step * group + n
            cross = kept[k] + arrived[k].astype(F32)
            if n == 0:
                cross = jnp.where(origin + k > 0, cross, 0.0)
            loaded.append(cross.astype(BF16))
        done = plane_transform(loaded, y_rows[...], mixes[...])
        size = group * cells
        tiles[pl.ds(pl.multiple_of(step * size, size), size), :] = done
        return carry

    lax.fori_loop(0, half // group, body, 0)
    low = lax.broadcasted_iota(jnp.int32, (padded, lanes), 1) < cells
    for y in range(0, cells, 2):
        even = tiles[pl.ds(y, padded, stride=cells), :]
        odd = tiles[pl.ds(y + 1, padded, stride=cells), :]
        where = slice(y * cells, y * cells + lanes)
        real = jnp.where(low, even, pltpu.roll(odd, cells, 1))
        imag = jnp.where(low, pltpu.roll(even, cells, 1), odd)
        lined[:, where] = jnp.concatenate([real, imag], axis=0).astype(BF16)
    best = None
    wide = 8 * lanes
    for block in range(cells * cells // wide):
        scores = jnp.dot(
            x_back[...], lined[:, block * wide : (block + 1) * wide], preferred_element_type=F32
        )
        for piece in range(wide // lanes):
            part = scores[:, piece * lanes : (piece + 1) * lanes]
            best = part if best is None else jnp.maximum(best, part)
    top = jnp.max(jnp.transpose(best), axis=0, keepdims=True)
    out[...] = top * (1.0 / (cells * math.sqrt(cells)))


def inverse(kept, arrived, tables, padded, after):
    half, cells, lanes = kept.shape
    return pl.pallas_call(
        lambda *refs: inverse_kernel(padded, *refs),
        out_shape=jax.ShapeDtypeStruct((1, cells), F32),
        in_specs=[vmem()] * 5 + [pl.BlockSpec(memory_space=pl.ANY)] * len(after),
        out_specs=vmem(),
        scratch_shapes=[
            pltpu.VMEM((padded * cells, lanes), F32),
            pltpu.VMEM((2 * padded, cells * cells), BF16),
        ],
        name="inverse_pair",
        compiler_params=pltpu.CompilerParams(vmem_limit_bytes=VMEM_BYTES),
        cost_estimate=pl.CostEstimate(
            flops=half * 6 * lanes * lanes * cells,
            bytes_accessed=half * cells * lanes * 16,
            transcendentals=0,
        ),
    )(kept, arrived, *tables, *after)


def marked(after):
    def kernel(*refs):
        refs[-1][...] = jnp.zeros_like(refs[-1])

    return pl.pallas_call(
        kernel,
        out_shape=jax.ShapeDtypeStruct((8, 128), F32),
        in_specs=[pl.BlockSpec(memory_space=pl.ANY)] * len(after),
        out_specs=vmem(),
        name="mark",
        compiler_params=pltpu.CompilerParams(vmem_limit_bytes=VMEM_BYTES),
        cost_estimate=pl.CostEstimate(flops=0, bytes_accessed=4096, transcendentals=0),
    )(*after)


def shards(receptor_occupancy, ligand_occupancy, rot_index, receptor_extent, channel_weight):
    channels = receptor_occupancy.shape[1]
    thickness = receptor_occupancy.shape[2]
    parts = lax.axis_size("fft")
    if parts != LIG_STEPS or channels % parts:
        raise ValueError("unsupported split")
    mine = channels // parts
    cells = thickness * parts
    half = cells // 2 + 1
    padded = -(-half // 8) * 8
    me = lax.axis_index("fft").astype(jnp.int32)
    forward_tables, backward_tables = make_tables(cells, half, padded)
    core = me[None]

    def other_channels(occupancy):
        theirs = lax.dynamic_slice_in_dim(occupancy[0], (1 - me) * mine, mine, 0)
        return passed_along(theirs.astype(BF16), "fft", 1)

    extents = [receptor_extent]
    for steps in range(1, REC_STEPS):
        extents.append(passed_along(receptor_extent, "rec", steps))
    receptor_in = other_channels(receptor_occupancy)
    ligand_in = other_channels(ligand_occupancy)

    def hopped(value, axis):
        return passed_along(value, axis, 1)

    def spectrum(rotated, channel, after):
        occupancy, received = (
            (ligand_occupancy, ligand_in) if rotated else (receptor_occupancy, receptor_in)
        )
        return forward(
            occupancy, received, core, rot_index, forward_tables, half, padded, rotated,
            channel, after,
        )

    receptor = []
    first = []
    for channel in range(mine):
        receptor.append(spectrum(False, channel, first[-1:]))
        first.append(spectrum(True, channel, receptor[-1:]))
    receptors = [receptor]
    for _ in range(1, REC_STEPS):
        receptors.append([hopped(each, "rec") for each in receptors[-1]])
    second = [hopped(each, "lig") for each in first]

    last = []
    for each in receptors[1]:
        last = [marked([each, *(last or first[-1:])])]

    def crossed(keep, step, after):
        return cross_part(keep, core, channel_weight, receptors[step], first, second, after)

    tops = [None] * REC_STEPS
    pending = []
    for step in (1, 0, *range(2, REC_STEPS)):
        sent = crossed(False, step, last)
        arrived = passed_along(sent, "fft", 1)
        kept = crossed(True, step, [sent])
        pending.append((step, kept, arrived))
        last = [kept]
        if step == 1:
            continue
        while pending:
            place, kept, arrived = pending.pop(0)
            tops[place] = inverse(kept, arrived, backward_tables, padded, last)
            last = [tops[place]]
    ours = jnp.concatenate(tops, axis=0)
    theirs = passed_along(ours, "fft", 1)
    start = me * thickness
    ours = lax.dynamic_slice_in_dim(ours, start, thickness, 1)
    theirs = lax.dynamic_slice_in_dim(theirs, start, thickness, 1)
    steps = jnp.arange(LIG_STEPS, dtype=jnp.int32)[None, :, None]
    both = jnp.where(steps == me, ours[:, None], theirs[:, None])
    planes = start + jnp.arange(thickness, dtype=jnp.int32)
    limit = jnp.concatenate(extents)[:, None, None]
    return jnp.where(planes[None, None, :] < limit, both, 0.0)[None]


def solution(mesh):
    placed = (
        P(("groups", "rec", "lig"), None, "fft", None),
        P(("groups", "rec", "lig"), None, "fft", None),
        P(("groups", "rec", "lig")),
        P(("groups", "rec", "lig")),
        P(),
    )

    return jax.shard_map(
        shards,
        mesh=mesh,
        in_specs=placed,
        out_specs=P(("groups", "rec", "lig"), None, None, "fft"),
        check_vma=False,
    )
```

```python
import math

import jax
import jax.numpy as jnp
import numpy as np
from jax import lax
from jax.experimental import pallas as pl
from jax.experimental.pallas import tpu as pltpu
from jax.sharding import PartitionSpec as P


REC_STEPS = 3
LIG_STEPS = 2
F32 = jnp.float32
BF16 = jnp.bfloat16
VMEM_BYTES = 20 * 1024 * 1024


def passed_along(value, axis, steps):
    count = lax.axis_size(axis)
    pairs = [(source, (source + steps) % count) for source in range(count)]
    return lax.ppermute(value, axis, pairs)


def trig_tables(cells):
    indices = np.arange(cells)
    phases = indices[:, None] * indices[None, :] % cells
    angles = phases.astype(np.float32) * np.float32(2.0 * math.pi / cells)
    return np.cos(angles), np.sin(angles)


def lane_mixes(real, imag):
    first = np.block([[real, imag], [-imag, real]])
    second = np.block([[-imag, real], [-real, -imag]])
    return np.concatenate([first, second], axis=0)


def make_tables(cells, half, padded):
    cosine, sine = trig_tables(cells)
    split = cells // 2
    x_rows = np.zeros((2 * padded, cells), np.float32)
    x_rows[:half] = cosine[:half]
    x_rows[padded : padded + half] = -sine[:half]
    x_swapped = np.concatenate([x_rows[:, split:], x_rows[:, :split]], axis=1)
    y_rows = np.concatenate([cosine, -sine], axis=0)
    forward = (
        np.stack([x_rows, x_swapped]),
        np.stack([y_rows, y_rows[:, ::-1]]),
        np.stack([lane_mixes(cosine, -sine), lane_mixes(cosine[::-1], -sine[::-1])]),
    )
    twice = np.full((half,), 2.0, np.float32)
    twice[0] = 1.0
    twice[-1] = 1.0
    x_back = np.zeros((cells, 2 * padded), np.float32)
    x_back[:, :half] = cosine[:, :half] * twice
    x_back[:, padded : padded + half] = -sine[:, :half] * twice
    backward = (
        x_back,
        np.concatenate([cosine, sine], axis=0),
        lane_mixes(cosine, sine),
    )
    return (
        tuple(jnp.asarray(table, BF16) for table in forward),
        tuple(jnp.asarray(table, BF16) for table in backward),
    )


def group_of(half):
    return max(size for size in range(1, 12) if half % size == 0)


def plane_transform(tiles, y_rows, mixes):
    cells, lanes = tiles[0].shape
    mixed = jnp.dot(y_rows, jnp.concatenate(tiles, axis=1), preferred_element_type=F32)
    mixed = mixed.astype(BF16)
    parts = [mixed[:, n * lanes : (n + 1) * lanes] for n in range(len(tiles))]
    real = jnp.concatenate([part[:cells] for part in parts], axis=0)
    imag = jnp.concatenate([part[cells:] for part in parts], axis=0)
    return jnp.dot(
        jnp.concatenate([real, imag], axis=1), mixes, preferred_element_type=F32
    )


def forward_kernel(
    half, padded, rotated, core, turns, own, received, x_rows, y_rows, mixes, *refs
):
    out, tiles = refs[-2:]
    cells = y_rows.shape[2]
    lanes = 2 * cells
    group = group_of(half)
    grid = jnp.concatenate([own[0, 0].astype(F32).astype(BF16), received[0]], axis=0)
    low = lax.broadcasted_iota(jnp.int32, (padded, lanes), 1) < cells
    wide = 8 * lanes
    for block in range(cells * cells // wide):
        rows = jnp.dot(
            x_rows[0], grid[:, block * wide : (block + 1) * wide], preferred_element_type=F32
        )
        for piece in range(wide // lanes):
            real = rows[:padded, piece * lanes : (piece + 1) * lanes]
            imag = rows[padded:, piece * lanes : (piece + 1) * lanes]
            y = 2 * (block * (wide // lanes) + piece)
            tiles[pl.ds(y, padded, stride=cells), :] = jnp.where(
                low, real, pltpu.roll(imag, cells, 1)
            )
            tiles[pl.ds(y + 1, padded, stride=cells), :] = jnp.where(
                low, pltpu.roll(real, cells, 1), imag
            )

    def tile_at(k):
        return pl.ds(pl.multiple_of(k * cells, cells), cells)

    if rotated:

        @pl.when(turns[0] % 2 == 1)
        def _():
            def turn(step, carry):
                for n in range(group):
                    where = tile_at(step * group + n)
                    turned = jnp.transpose(tiles[where, :])
                    tiles[where, :] = jnp.concatenate([turned[:cells], turned[cells:]], axis=1)
                return carry

            lax.fori_loop(0, half // group, turn, 0)

    def body(step, carry):
        loaded = [tiles[tile_at(step * group + n), :].astype(BF16) for n in range(group)]
        done = plane_transform(loaded, y_rows[0], mixes[0])
        out[pl.ds(step * group, group)] = done.astype(BF16).reshape(group, cells, lanes)
        return carry

    lax.fori_loop(0, half // group, body, 0)


def forward(occupancy, received, core, turns, tables, half, padded, rotated, channel, after):
    mine, thickness, plane = received.shape
    cells = tables[1].shape[2]
    lanes = 2 * cells

    def y_reversed(turns):
        return (((turns[0] + 1) % 4) // 2 if rotated else 0, 0, 0)

    def z_reversed(turns):
        return (turns[0] // 2 if rotated else 0, 0, 0)

    grid_spec = pltpu.PrefetchScalarGridSpec(
        num_scalar_prefetch=2,
        grid=(1,),
        in_specs=[
            pl.BlockSpec((1, 1, thickness, plane), lambda c, f, t: (0, f[0] * mine + channel, 0, 0)),
            pl.BlockSpec((1, thickness, plane), lambda c, f, t: (channel, 0, 0)),
            pl.BlockSpec((1, 2 * padded, cells), lambda c, f, t: (f[0], 0, 0)),
            pl.BlockSpec((1, lanes, cells), lambda c, f, t: y_reversed(t)),
            pl.BlockSpec((1, 2 * lanes, lanes), lambda c, f, t: z_reversed(t)),
        ]
        + [pl.BlockSpec(memory_space=pl.ANY)] * len(after),
        out_specs=pl.BlockSpec((half, cells, lanes), lambda c, f, t: (0, 0, 0)),
        scratch_shapes=[pltpu.VMEM((padded * cells, lanes), F32)],
    )
    return pl.pallas_call(
        lambda *refs: forward_kernel(half, padded, rotated, *refs),
        out_shape=jax.ShapeDtypeStruct((half, cells, lanes), BF16),
        grid_spec=grid_spec,
        name="forward_pose" if rotated else "forward_receptor",
        compiler_params=pltpu.CompilerParams(vmem_limit_bytes=VMEM_BYTES),
        cost_estimate=pl.CostEstimate(
            flops=half * 6 * lanes * lanes * cells,
            bytes_accessed=plane * thickness * 20,
            transcendentals=0,
        ),
    )(core, turns, occupancy, received, *tables, *after)


def partial_cross(scales, receptors, ligands, exchange, where, cells):
    same = None
    swapped = None
    for scale, receptor, ligand in zip(scales, receptors, ligands):
        left = receptor[where].astype(F32) * scale
        right = ligand(where)
        turned = jnp.dot(right, exchange, preferred_element_type=F32)
        right = right.astype(F32)
        same = left * right if same is None else same + left * right
        swapped = left * turned if swapped is None else swapped + left * turned
    axis = same.ndim - 1
    low = lax.broadcasted_iota(jnp.int32, same.shape, axis) < cells
    across = pltpu.roll(jnp.where(low, -swapped, same), cells, axis)
    return jnp.where(low, same, swapped) + across


def chosen(pick_second, first, second):
    return lambda where: jnp.where(pick_second, second[where], first[where])


def cross_kernel(mine, keep, core, weights, *refs):
    receptors, firsts, seconds = refs[:mine], refs[mine : 2 * mine], refs[2 * mine : 3 * mine]
    out = refs[-1]
    group, cells, lanes = out.shape
    volume = 1.0 / float(cells) ** 3
    scales = [weights[core[0] * mine + c] * volume for c in range(mine)]
    second = core[0] == int(keep)
    ligands = [chosen(second, *pair) for pair in zip(firsts, seconds)]

    row = lax.broadcasted_iota(jnp.int32, (lanes, lanes), 0)
    column = lax.broadcasted_iota(jnp.int32, (lanes, lanes), 1)
    exchange = jnp.where((row + cells) % lanes == column, 1.0, 0.0).astype(BF16)
    for k in range(group):
        out[k] = partial_cross(scales, receptors, ligands, exchange, k, cells).astype(out.dtype)


def vmem():
    return pl.BlockSpec(memory_space=pltpu.VMEM)


def smem():
    return pl.BlockSpec(memory_space=pltpu.SMEM)


def cross_part(keep, core, weights, receptor, first, second, after):
    mine = len(receptor)
    half, cells, lanes = receptor[0].shape
    group = group_of(half)
    block = (group, cells, lanes)

    def used(is_second):
        def index(k, core):
            wanted = int(keep) if is_second else int(not keep)
            return (jnp.where(core[0] == wanted, k, 0), 0, 0)

        return pl.BlockSpec(block, index)

    grid_spec = pltpu.PrefetchScalarGridSpec(
        num_scalar_prefetch=1,
        grid=(half // group,),
        in_specs=[smem()]
        + [pl.BlockSpec(block, lambda k, core: (k, 0, 0))] * mine
        + [used(False)] * mine
        + [used(True)] * mine
        + [pl.BlockSpec(memory_space=pl.ANY)] * len(after),
        out_specs=pl.BlockSpec(block, lambda k, core: (k, 0, 0)),
    )
    return pl.pallas_call(
        lambda *refs: cross_kernel(mine, keep, *refs),
        out_shape=jax.ShapeDtypeStruct((half, cells, lanes), F32 if keep else BF16),
        grid_spec=grid_spec,
        name="cross_keep" if keep else "cross_send",
        compiler_params=pltpu.CompilerParams(vmem_limit_bytes=VMEM_BYTES),
        cost_estimate=pl.CostEstimate(
            flops=mine * half * cells * lanes * 10,
            bytes_accessed=half * cells * lanes * 14,
            transcendentals=0,
        ),
    )(core, weights, *receptor, *first, *second, *after)


def inverse_kernel(padded, kept, arrived, x_back, y_rows, mixes, *refs):
    out, tiles, lined = refs[-3:]
    half, cells, lanes = kept.shape
    group = group_of(half)
    tiles[half * cells :, :] = jnp.zeros(((padded - half) * cells, lanes), F32)
    row = lax.broadcasted_iota(jnp.int32, (cells, lanes), 0)
    lane = lax.broadcasted_iota(jnp.int32, (cells, lanes), 1) % cells
    origin = row + lane

    def body(step, carry):
        loaded = []
        for n in range(group):
            k = step * group + n
            cross = kept[k] + arrived[k].astype(F32)
            if n == 0:
                cross = jnp.where(origin + k > 0, cross, 0.0)
            loaded.append(cross.astype(BF16))
        done = plane_transform(loaded, y_rows[...], mixes[...])
        size = group * cells
        tiles[pl.ds(pl.multiple_of(step * size, size), size), :] = done
        return carry

    lax.fori_loop(0, half // group, body, 0)
    low = lax.broadcasted_iota(jnp.int32, (padded, lanes), 1) < cells
    for y in range(0, cells, 2):
        even = tiles[pl.ds(y, padded, stride=cells), :]
        odd = tiles[pl.ds(y + 1, padded, stride=cells), :]
        where = slice(y * cells, y * cells + lanes)
        real = jnp.where(low, even, pltpu.roll(odd, cells, 1))
        imag = jnp.where(low, pltpu.roll(even, cells, 1), odd)
        lined[:, where] = jnp.concatenate([real, imag], axis=0).astype(BF16)
    best = None
    wide = 8 * lanes
    for block in range(cells * cells // wide):
        scores = jnp.dot(
            x_back[...], lined[:, block * wide : (block + 1) * wide], preferred_element_type=F32
        )
        for piece in range(wide // lanes):
            part = scores[:, piece * lanes : (piece + 1) * lanes]
            best = part if best is None else jnp.maximum(best, part)
    top = jnp.max(jnp.transpose(best), axis=0, keepdims=True)
    out[...] = top * (1.0 / (cells * math.sqrt(cells)))


def inverse(kept, arrived, tables, padded, after):
    half, cells, lanes = kept.shape
    return pl.pallas_call(
        lambda *refs: inverse_kernel(padded, *refs),
        out_shape=jax.ShapeDtypeStruct((1, cells), F32),
        in_specs=[vmem()] * 5 + [pl.BlockSpec(memory_space=pl.ANY)] * len(after),
        out_specs=vmem(),
        scratch_shapes=[
            pltpu.VMEM((padded * cells, lanes), F32),
            pltpu.VMEM((2 * padded, cells * cells), BF16),
        ],
        name="inverse_pair",
        compiler_params=pltpu.CompilerParams(vmem_limit_bytes=VMEM_BYTES),
        cost_estimate=pl.CostEstimate(
            flops=half * 6 * lanes * lanes * cells,
            bytes_accessed=half * cells * lanes * 16,
            transcendentals=0,
        ),
    )(kept, arrived, *tables, *after)


def marked(after):
    def kernel(*refs):
        refs[-1][...] = jnp.zeros_like(refs[-1])

    return pl.pallas_call(
        kernel,
        out_shape=jax.ShapeDtypeStruct((8, 128), F32),
        in_specs=[pl.BlockSpec(memory_space=pl.ANY)] * len(after),
        out_specs=vmem(),
        name="mark",
        compiler_params=pltpu.CompilerParams(vmem_limit_bytes=VMEM_BYTES),
        cost_estimate=pl.CostEstimate(flops=0, bytes_accessed=4096, transcendentals=0),
    )(*after)


def shards(receptor_occupancy, ligand_occupancy, rot_index, receptor_extent, channel_weight):
    channels = receptor_occupancy.shape[1]
    thickness = receptor_occupancy.shape[2]
    parts = lax.axis_size("fft")
    if parts != LIG_STEPS or channels % parts:
        raise ValueError("unsupported split")
    mine = channels // parts
    cells = thickness * parts
    half = cells // 2 + 1
    padded = -(-half // 8) * 8
    me = lax.axis_index("fft").astype(jnp.int32)
    forward_tables, backward_tables = make_tables(cells, half, padded)
    core = me[None]

    def other_channels(occupancy):
        theirs = lax.dynamic_slice_in_dim(occupancy[0], (1 - me) * mine, mine, 0)
        return passed_along(theirs.astype(BF16), "fft", 1)

    extents = [receptor_extent]
    for steps in range(1, REC_STEPS):
        extents.append(passed_along(receptor_extent, "rec", steps))
    receptor_in = other_channels(receptor_occupancy)
    ligand_in = other_channels(ligand_occupancy)

    def hopped(value, axis):
        return passed_along(value, axis, 1)

    def spectrum(rotated, channel, after):
        occupancy, received = (
            (ligand_occupancy, ligand_in) if rotated else (receptor_occupancy, receptor_in)
        )
        return forward(
            occupancy, received, core, rot_index, forward_tables, half, padded, rotated,
            channel, after,
        )

    receptor = []
    first = []
    for channel in range(mine):
        receptor.append(spectrum(False, channel, first[-1:]))
        first.append(spectrum(True, channel, receptor[-1:]))
    receptors = [receptor]
    for _ in range(1, REC_STEPS):
        receptors.append([hopped(each, "rec") for each in receptors[-1]])
    second = [hopped(each, "lig") for each in first]

    last = []
    for each in receptors[1]:
        last = [marked([each, *(last or first[-1:])])]

    def crossed(keep, step, after):
        return cross_part(keep, core, channel_weight, receptors[step], first, second, after)

    tops = [None] * REC_STEPS
    pending = []
    for step in (1, 0, *range(2, REC_STEPS)):
        sent = crossed(False, step, last)
        arrived = passed_along(sent, "fft", 1)
        kept = crossed(True, step, [sent])
        pending.append((step, kept, arrived))
        last = [kept]
        if step == 1:
            continue
        while pending:
            place, kept, arrived = pending.pop(0)
            tops[place] = inverse(kept, arrived, backward_tables, padded, last)
            last = [tops[place]]
    ours = jnp.concatenate(tops, axis=0)
    theirs = passed_along(ours, "fft", 1)
    start = me * thickness
    ours = lax.dynamic_slice_in_dim(ours, start, thickness, 1)
    theirs = lax.dynamic_slice_in_dim(theirs, start, thickness, 1)
    steps = jnp.arange(LIG_STEPS, dtype=jnp.int32)[None, :, None]
    both = jnp.where(steps == me, ours[:, None], theirs[:, None])
    planes = start + jnp.arange(thickness, dtype=jnp.int32)
    limit = jnp.concatenate(extents)[:, None, None]
    return jnp.where(planes[None, None, :] < limit, both, 0.0)[None]


def solution(mesh):
    placed = (
        P(("groups", "rec", "lig"), None, "fft", None),
        P(("groups", "rec", "lig"), None, "fft", None),
        P(("groups", "rec", "lig")),
        P(("groups", "rec", "lig")),
        P(),
    )

    return jax.shard_map(
        shards,
        mesh=mesh,
        in_specs=placed,
        out_specs=P(("groups", "rec", "lig"), None, None, "fft"),
        check_vma=False,
    )
```
